32 devices in a mesh: ctx: 16 (over z, y, core), section: 2 (over x).
Axes of the slice: x: 2, y: 2, z: 4, core: 2. Of those that a mesh axis runs over, the one named last changes fastest.
Arguments:
- queries: bfloat16 [2, 2048, 2560], P('section', 'ctx'), may hold values from -80 to 80
- grad_out: bfloat16 [2, 2048, 2560], P('section', 'ctx'), may hold values from -6 to 6
- keys_values: bfloat16 [2, 2048, 512], P(None, 'ctx'), may hold values from -16 to 16
- doc_ids: int32 [2048], replicated, may hold values from 0 to 7, never falling along the last dimension, each value on 1 to 512 neighbouring positions
Outputs:
- grad_queries: bfloat16 [2, 2048, 2560], P('section', 'ctx')
- grad_kv: bfloat16 [2, 2048, 512], P(None, ('ctx', 'section'))
The draws below stay inside these ranges and needn't reach their ends.
Inputs may be any that keep to these rules, and one draw needn't show every extreme that they name: `doc_ids`: document numbers never fall along the sequence; a document has at most 512 tokens.
All inputs are finite; a program needn't handle non-finite values.
Results may differ from the reference program's by a relative error of at most 0.015.
Values may be sent and summed in bfloat16 or wider, within the bound.
A program may use at most 64 MiB of HBM per device.

```python
import math
import jax
import jax.numpy as jnp
import numpy as np
from jax import lax

HD = 128
KVH = 4
GROUP = 5
TOKENS = 2048
LAYERS = 2
HEADS = 20


def cache_base(key):
    keys = jnp.clip(jax.random.normal(jax.random.fold_in(key, 11), (TOKENS, KVH, HD), jnp.float32), -5.0, 5.0)
    values = jnp.clip(jax.random.normal(jax.random.fold_in(key, 12), (TOKENS, KVH, HD), jnp.float32), -5.0, 5.0)
    return (keys, values)


def draw_keys_values(key, part):
    keys, values = cache_base(key)
    return jnp.stack([keys, values]).reshape(2, TOKENS, KVH * HD).astype(jnp.bfloat16)


def draw_queries(key, part):
    shaped = jnp.clip(jax.random.normal(jax.random.fold_in(key, 13), (LAYERS, TOKENS, KVH, GROUP, HD), jnp.float32), -5.0, 5.0)
    return shaped.reshape(LAYERS, TOKENS, KVH * GROUP * HD).astype(jnp.bfloat16)


def level_of(stream_key, dims, cuts, smallest, top_value):
    loudness = 1.0
    for axis_at, shards_of in cuts:
        steps = jax.random.uniform(jax.random.fold_in(jax.random.fold_in(stream_key, 6), axis_at), (shards_of,), jnp.float32, smallest / len(cuts), top_value / len(cuts))
        loudness = loudness * jnp.repeat(jnp.exp(steps), dims[axis_at] // shards_of).reshape((-1,) + (1,) * (len(dims) - 1 - axis_at))
    return loudness


def split_up(number_of, total, reach, lean):
    portions = [(1 << 20) // math.isqrt(standing ** lean) + 1 for standing in range(2, number_of + 1)]
    spare, holding = total - reach - (number_of - 1), [1] * (number_of - 1)
    while spare > 0:
        free = [i for i in range(number_of - 1) if holding[i] < reach]
        mass, budget = sum([portions[i] for i in free]), spare
        for i in free:
            addition = min(reach - holding[i], max(1, budget * portions[i] // mass), spare)
            holding[i] = holding[i] + addition
            spare = spare - addition
    return np.array([reach] + holding)


def ragged_sizes(stream_key, amount, total, reach, lean):
    if amount == 2:
        one = jax.random.randint(stream_key, (), max(1, total - reach), min(reach, total - 1) + 1)
        return jnp.stack([one, total - one])
    lengths = jnp.asarray(split_up(amount, total, reach, lean), jnp.int32)
    twos = (amount - 1) // 2
    giver, receiver = lengths[1:1 + 2 * twos:2], lengths[2:2 + 2 * twos:2]
    room = jnp.minimum(giver - 1, reach - receiver)
    moved = jax.random.randint(jax.random.fold_in(stream_key, 1), (twos,), 0, 1 << 20) % (room + 1)
    lengths = lengths.at[1:1 + 2 * twos:2].set(giver - moved).at[2:2 + 2 * twos:2].set(receiver + moved)
    return lengths[jax.random.permutation(jax.random.fold_in(stream_key, 2), amount)]


def noise(own_key, dims, spread, limit, split=(), kind=jnp.bfloat16):
    result = jax.random.normal(own_key, dims, jnp.float32) * spread
    if len(split) > 0:
        result = level_of(own_key, dims, split, -0.22, 0.18) * result
    return jnp.clip(result, min=-limit, max=limit).astype(kind)


def setup_inputs(seed: int = 0) -> dict:
    streams_of = jax.random.split(jax.random.key(seed), 5)
    queries = draw_queries(jax.random.fold_in(streams_of[4], 71), 0)
    grad_out = noise(streams_of[1], (LAYERS, TOKENS, HEADS * HD), 1.0, 6.0, ((0, 2), (1, 16)))
    keys_values = draw_keys_values(jax.random.fold_in(streams_of[4], 71), 0)
    doc_ids = jnp.searchsorted(jnp.cumsum(ragged_sizes(streams_of[3], 8, TOKENS, TOKENS // 4, 1)), jnp.arange(TOKENS), side="right").astype(jnp.int32)
    return {"queries": queries, "grad_out": grad_out, "keys_values": keys_values, "doc_ids": doc_ids}


def reference(queries, grad_out, keys_values, doc_ids):
    scale = HD ** -0.5
    keys = keys_values[0].reshape(TOKENS, KVH, HD).astype(jnp.float32)
    values = keys_values[1].reshape(TOKENS, KVH, HD).astype(jnp.float32)
    qblock = min(512, TOKENS)
    nblocks = TOKENS // qblock
    places = jnp.arange(TOKENS, dtype=jnp.int32)

    def one_block(carry, index):
        layer = index // nblocks
        start = (index % nblocks) * qblock
        qrows = lax.dynamic_slice_in_dim(queries[layer], start, qblock, 0).reshape(qblock, KVH, GROUP, HD).astype(jnp.float32)
        grows = lax.dynamic_slice_in_dim(grad_out[layer], start, qblock, 0).reshape(qblock, KVH, GROUP, HD).astype(jnp.float32)
        qplace = start + jnp.arange(qblock, dtype=jnp.int32)
        qdoc = lax.dynamic_slice_in_dim(doc_ids, start, qblock, 0)
        visible = (places[None, :] <= qplace[:, None]) & (doc_ids[None, :] == qdoc[:, None])
        seen = visible[:, None, None, :]
        scores = jnp.einsum("rgnd,kgd->rgnk", qrows, keys) * scale
        scores = jnp.where(seen, scores, -1e30)
        top = jnp.max(scores, axis=-1)
        lse = top + jnp.log(jnp.sum(jnp.exp(scores - top[..., None]), axis=-1))
        weights = jnp.where(seen, jnp.exp(scores - lse[..., None]), 0.0)
        out = jnp.einsum("rgnk,kgd->rgnd", weights, values, precision=lax.Precision.HIGHEST)
        delta = jnp.sum(grows * out, axis=-1)
        prob = weights.astype(jnp.bfloat16).astype(jnp.float32)
        dprob = jnp.einsum("rgnd,kgd->rgnk", grows, values)
        dscore = (prob * (dprob - delta[..., None])).astype(jnp.bfloat16).astype(jnp.float32)
        dquery = (scale * jnp.einsum("rgnk,kgd->rgnd", dscore, keys)).astype(jnp.bfloat16)
        dkeys = scale * jnp.einsum("rgnk,rgnd->kgd", dscore, qrows)
        dvalues = jnp.einsum("rgnk,rgnd->kgd", prob, grows)
        return (carry[0] + dkeys, carry[1] + dvalues), dquery.reshape(qblock, HEADS * HD)

    start_sums = (jnp.zeros((TOKENS, KVH, HD), jnp.float32), jnp.zeros((TOKENS, KVH, HD), jnp.float32))
    sums, dqueries = lax.scan(one_block, start_sums, jnp.arange(LAYERS * nblocks, dtype=jnp.int32))
    grad_queries = dqueries.reshape(LAYERS, TOKENS, HEADS * HD)
    grad_kv = jnp.stack([sums[0], sums[1]]).reshape(2, TOKENS, KVH * HD).astype(jnp.bfloat16)
    return grad_queries, grad_kv
```

```python
import functools

import jax
import jax.numpy as jnp
from jax import lax
from jax.experimental import pallas as pl
from jax.experimental.pallas import tpu as pltpu
from jax.sharding import PartitionSpec as P

HD = 128
MESH = pl.DeviceIdType.MESH
LOG2E = 1.4426950408889634
NEG = -1e30


def kernel(
    n, sections, reach, heads_kv, group,
    q_ref, do_ref, kv_ref, docs_ref,
    dq_ref, out_ref,
    qbuf, dobuf, kvbuf, bias, pbuf, dsbuf, acc, sbuf, rbuf, dqbuf,
    lsem, qsend, qrecv, kvsend, kvrecv, gsend, grecv, dqsend, dqrecv, dqloc,
):
    me = lax.axis_index("ctx")
    sec = lax.axis_index("section")
    layers, rows = q_ref.shape[0], q_ref.shape[1]
    core = lax.rem(me, 2)
    other = 1 - core
    chip = me // 2
    chips = n // 2
    depth = reach // 2
    blocks = reach + 2
    heads = heads_kv // 2
    gw = group * HD
    window = (reach + 1) * rows
    piece = rows // sections
    scale = HD ** (-0.5)

    def dev(ctx, section):
        return {"ctx": ctx, "section": section}

    def cols(head, width):
        return pl.ds(pl.multiple_of(head * width, HD), width)

    def local_copies(h):
        g = core * heads + h
        return [
            pltpu.make_async_copy(q_ref.at[:, :, cols(g, gw)], qbuf.at[h, core], lsem.at[h, 0]),
            pltpu.make_async_copy(do_ref.at[:, :, cols(g, gw)], dobuf.at[h, core], lsem.at[h, 1]),
            pltpu.make_async_copy(
                kv_ref.at[:, :, cols(g, HD)], kvbuf.at[h, :, reach + core], lsem.at[h, 2]
            ),
        ]

    def q_copies(h):
        g = other * heads + h
        partner = dev(2 * chip + other, sec)
        return [
            pltpu.make_async_remote_copy(
                src_ref=src.at[:, :, cols(g, gw)], dst_ref=dst.at[h, core],
                send_sem=qsend.at[h, k], recv_sem=qrecv.at[h, k],
                device_id=partner, device_id_type=MESH,
            )
            for k, (src, dst) in enumerate([(q_ref, qbuf), (do_ref, dobuf)])
        ]

    def kv_copy(h, d, w):
        to = lax.rem(core + w, 2)
        slot = core - 2 * d + reach
        return pltpu.make_async_remote_copy(
            src_ref=kv_ref.at[:, :, cols(to * heads + h, HD)], dst_ref=kvbuf.at[h, :, slot],
            send_sem=kvsend.at[h, d, w], recv_sem=kvrecv.at[h, slot],
            device_id=dev(2 * (chip + d) + to, sec), device_id_type=MESH,
        )

    def kv_wait(h, slot):
        return pltpu.make_async_remote_copy(
            src_ref=kv_ref.at[:, :, pl.ds(0, HD)], dst_ref=kvbuf.at[h, :, slot],
            send_sem=kvsend.at[h, 0, 0], recv_sem=kvrecv.at[h, slot],
            device_id=dev(2 * chip + other, sec), device_id_type=MESH,
        )

    def g_copy(h, slot, t):
        d = (reach + 1 - slot) // 2
        owner_core = (slot - reach) % 2
        to = lax.rem(sec + t, sections)
        return pltpu.make_async_remote_copy(
            src_ref=sbuf.at[h, slot, :, pl.ds(pl.multiple_of(to * piece, piece), piece)],
            dst_ref=rbuf.at[d, sec, core, h],
            send_sem=gsend.at[h, slot, t], recv_sem=grecv.at[d, sec, core, h],
            device_id=dev(2 * (chip - d) + owner_core, to), device_id_type=MESH,
        )

    def g_wait(h, d, s, c):
        return pltpu.make_async_remote_copy(
            src_ref=sbuf.at[h, 0, :, pl.ds(0, piece)], dst_ref=rbuf.at[d, s, c, h],
            send_sem=gsend.at[h, 0, 0], recv_sem=grecv.at[d, s, c, h],
            device_id=dev(2 * chip + other, sec), device_id_type=MESH,
        )

    def dq_copy(h):
        return pltpu.make_async_remote_copy(
            src_ref=dqbuf.at[h, other], dst_ref=dq_ref.at[:, :, cols(core * heads + h, gw)],
            send_sem=dqsend.at[h], recv_sem=dqrecv.at[h],
            device_id=dev(2 * chip + other, sec), device_id_type=MESH,
        )

    def dq_wait(h):
        return pltpu.make_async_remote_copy(
            src_ref=dqbuf.at[h, other], dst_ref=dq_ref.at[:, :, cols(other * heads + h, gw)],
            send_sem=dqsend.at[h], recv_sem=dqrecv.at[h],
            device_id=dev(2 * chip + other, sec), device_id_type=MESH,
        )

    def dq_local(h):
        return pltpu.make_async_copy(
            dqbuf.at[h, core], dq_ref.at[:, :, cols(core * heads + h, gw)], dqloc.at[h]
        )

    barrier = pltpu.get_barrier_semaphore()
    for step in range(-depth, depth + 1):
        @pl.when((chip + step >= 0) & (chip + step < chips))
        def _():
            for w in range(2):
                for t in range(sections):
                    if step == 0 and w == 0 and t == 0:
                        continue
                    pl.semaphore_signal(
                        barrier, inc=1,
                        device_id=dev(2 * (chip + step) + lax.rem(core + w, 2), lax.rem(sec + t, sections)),
                        device_id_type=MESH,
                    )

    for h in range(heads):
        for copy in local_copies(h):
            copy.start()

    near = jnp.minimum(chip, depth) + jnp.minimum(chips - 1 - chip, depth) + 1
    pl.semaphore_wait(barrier, near * (2 * sections) - 1)

    for h in range(heads):
        for d in range(depth, 0, -1):
            @pl.when(chip + d < chips)
            def _():
                for w in range(2):
                    kv_copy(h, d, w).start()
        kv_copy(h, 0, 1).start()
        for copy in q_copies(h):
            copy.start()

    for d in range(1, depth + 1):
        @pl.when(chip - d < 0)
        def _():
            for slot in (reach - 2 * d, reach - 2 * d + 1):
                for h in range(heads):
                    kvbuf[h, :, slot] = jnp.zeros((2, rows, HD), jnp.bfloat16)

        @pl.when(chip + d >= chips)
        def _():
            rbuf[d] = jnp.zeros(rbuf.shape[1:], jnp.bfloat16)

    row_at = lax.broadcasted_iota(jnp.int32, (rows, rows), 0)
    col_at = lax.broadcasted_iota(jnp.int32, (rows, rows), 1)
    for slot in range(blocks):
        at = 2 * chip - reach + slot
        kdoc = docs_ref[pl.ds(jnp.maximum(at, 0), 1), :].astype(jnp.float32)
        kdoc = jnp.transpose(jnp.broadcast_to(kdoc, (rows, rows)))
        for sub in range(2):
            if not 0 <= slot - sub <= reach:
                continue
            qdoc = docs_ref[pl.ds(2 * chip + sub, 1), :].astype(jnp.float32)
            kplace = at * rows + row_at
            qplace = (2 * chip + sub) * rows + col_at
            seen = (kplace <= qplace) & (kplace >= 0) & (kdoc == qdoc)
            bias[sub, (slot - sub) * rows : (slot - sub + 1) * rows] = jnp.where(seen, 0.0, NEG)

    def head_step(h, unused):
        local_copies(h)[2].wait()
        for slot in range(blocks):
            at = 2 * chip - reach + slot
            if slot < reach:
                condition = at >= 0
            else:
                condition = core != slot - reach

            @pl.when(condition)
            def _():
                kv_wait(h, slot).wait_recv()

        acc[...] = jnp.zeros_like(acc)

        def sub_step(w, unused):
            sub = lax.rem(core + w, 2)

            @pl.when(w == 0)
            def _():
                for copy in local_copies(h)[:2]:
                    copy.wait()

            @pl.when(w == 1)
            def _():
                for copy in q_copies(h):
                    copy.wait_recv()

            k = kvbuf[h, 0, pl.ds(sub, reach + 1)].reshape(window, HD)
            v = kvbuf[h, 1, pl.ds(sub, reach + 1)].reshape(window, HD)
            kt = jnp.transpose(k)
            keys_at = pl.ds(pl.multiple_of(sub * rows, rows), window)
            for layer in range(layers):
                for i in range(group):
                    at = pl.ds(i * HD, HD)
                    q = qbuf[h, sub, layer, :, at]
                    do = dobuf[h, sub, layer, :, at]
                    nt = (((1,), (1,)), ((), ()))
                    s = lax.dot_general(k, q, nt, preferred_element_type=jnp.float32)
                    dp = lax.dot_general(v, do, nt, preferred_element_type=jnp.float32)
                    s = s * (scale * LOG2E) + bias[sub]
                    e = jnp.exp2(s - jnp.max(s, axis=0, keepdims=True))
                    inverse = 1.0 / jnp.sum(e, axis=0, keepdims=True)
                    delta = jnp.sum(e * dp, axis=0, keepdims=True) * inverse
                    p = (e * inverse).astype(jnp.bfloat16)
                    pbuf[:, i * rows : (i + 1) * rows] = p
                    dsbuf[:, i * rows : (i + 1) * rows] = (
                        p.astype(jnp.float32) * (dp - delta)
                    ).astype(jnp.bfloat16)
                stack_q = jnp.concatenate(
                    [qbuf[h, sub, layer, :, i * HD : (i + 1) * HD] for i in range(group)], axis=0
                )
                stack_do = jnp.concatenate(
                    [dobuf[h, sub, layer, :, i * HD : (i + 1) * HD] for i in range(group)], axis=0
                )
                acc[0, keys_at] += jnp.dot(dsbuf[...], stack_q, preferred_element_type=jnp.float32)
                acc[1, keys_at] += jnp.dot(pbuf[...], stack_do, preferred_element_type=jnp.float32)
                dqt = jnp.dot(kt, dsbuf[...], preferred_element_type=jnp.float32) * scale
                for i in range(group):
                    dqbuf[h, sub, layer, :, i * HD : (i + 1) * HD] = jnp.transpose(
                        dqt[:, i * rows : (i + 1) * rows]
                    ).astype(jnp.bfloat16)
            return unused

        lax.fori_loop(0, 2, sub_step, 0)

        for slot in range(blocks):
            at = slice(slot * rows, (slot + 1) * rows)
            sbuf[h, slot, 0] = (acc[0, at] * scale).astype(jnp.bfloat16)
            sbuf[h, slot, 1] = acc[1, at].astype(jnp.bfloat16)
        own = pl.ds(pl.multiple_of(sec * piece, piece), piece)
        rbuf[0, sec, core, h] = sbuf[h, reach + core, :, own]
        for slot in range(blocks):
            for t in range(sections):
                if slot < reach:
                    condition = 2 * chip - reach + slot >= 0
                elif t == 0:
                    condition = core != slot - reach
                else:
                    condition = None
                if condition is None:
                    g_copy(h, slot, t).start()
                else:
                    pl.when(condition)(lambda: g_copy(h, slot, t).start())
        dq_copy(h).start()
        dq_local(h).start()
        return unused

    lax.fori_loop(0, heads, head_step, 0)

    for h in range(heads):
        for d in range(depth + 1):
            for s in range(sections):
                for c in range(2):
                    if d == 0:
                        condition = (sec != s) | (core != c)
                    else:
                        condition = chip + d < chips

                    @pl.when(condition)
                    def _():
                        g_wait(h, d, s, c).wait_recv()
    for c in range(2):
        for h in range(heads):
            total = None
            for d in range(depth + 1):
                for s in range(sections):
                    term = rbuf[d, s, c, h].astype(jnp.float32)
                    total = term if total is None else total + term
            g = c * heads + h
            out_ref[:, :, g * HD : (g + 1) * HD] = total.astype(jnp.bfloat16)

    def finish(h, unused):
        dq_wait(h).wait_recv()
        dq_copy(h).wait_send()
        dq_local(h).wait()
        for copy in q_copies(h):
            copy.wait_send()
        kv_copy(h, 0, 1).wait_send()
        for d in range(1, depth + 1):
            @pl.when(chip + d < chips)
            def _():
                for w in range(2):
                    kv_copy(h, d, w).wait_send()
        for slot in range(blocks):
            for t in range(sections):
                if slot < reach:
                    condition = 2 * chip - reach + slot >= 0
                elif t == 0:
                    condition = core != slot - reach
                else:
                    condition = None
                if condition is None:
                    g_copy(h, slot, t).wait_send()
                else:
                    pl.when(condition)(lambda: g_copy(h, slot, t).wait_send())
        return unused

    lax.fori_loop(0, heads, finish, 0)


def body(queries, grad_out, keys_values, doc_ids):
    layers, rows, width = queries.shape
    kv_width = keys_values.shape[2]
    heads_kv = kv_width // HD
    group = width // kv_width
    n = lax.axis_size("ctx")
    sections = lax.axis_size("section")
    reach = n // 4
    heads = heads_kv // 2
    blocks = reach + 2
    window = (reach + 1) * rows
    piece = rows // sections
    depth = reach // 2
    bf, f32 = jnp.bfloat16, jnp.float32
    dma = pltpu.SemaphoreType.DMA
    hbm = pl.BlockSpec(memory_space=pl.ANY)
    vmem = pl.BlockSpec(memory_space=pltpu.VMEM)
    return pl.pallas_call(
        functools.partial(kernel, n, sections, reach, heads_kv, group),
        out_shape=(
            jax.ShapeDtypeStruct(queries.shape, bf),
            jax.ShapeDtypeStruct((2, piece, kv_width), bf),
        ),
        in_specs=[hbm, hbm, hbm, vmem],
        out_specs=(hbm, vmem),
        scratch_shapes=[
            pltpu.VMEM((heads, 2, layers, rows, group * HD), bf),
            pltpu.VMEM((heads, 2, layers, rows, group * HD), bf),
            pltpu.VMEM((heads, 2, blocks, rows, HD), bf),
            pltpu.VMEM((2, window, rows), f32),
            pltpu.VMEM((window, group * rows), bf),
            pltpu.VMEM((window, group * rows), bf),
            pltpu.VMEM((2, blocks * rows, HD), f32),
            pltpu.VMEM((heads, blocks, 2, rows, HD), bf),
            pltpu.VMEM((depth + 1, sections, 2, heads, 2, piece, HD), bf),
            pltpu.VMEM((heads, 2, layers, rows, group * HD), bf),
            dma((heads, 3)),
            dma((heads, 2)),
            dma((heads, 2)),
            dma((heads, depth + 1, 2)),
            dma((heads, blocks)),
            dma((heads, blocks, sections)),
            dma((depth + 1, sections, 2, heads)),
            dma((heads,)),
            dma((heads,)),
            dma((heads,)),
        ],
        compiler_params=pltpu.CompilerParams(
            collective_id=0, has_side_effects=True, vmem_limit_bytes=48 * 1024 * 1024
        ),
        name="cross_backward",
    )(queries, grad_out, keys_values, doc_ids.reshape(-1, rows))


def solution(mesh):
    return jax.shard_map(
        body,
        mesh=mesh,
        in_specs=(P("section", "ctx", None), P("section", "ctx", None), P(None, "ctx", None), P()),
        out_specs=(P("section", "ctx", None), P(None, ("ctx", "section"), None)),
        check_vma=False,
    )
```

```python
import functools

import jax
import jax.numpy as jnp
from jax import lax
from jax.experimental import pallas as pl
from jax.experimental.pallas import tpu as pltpu
from jax.sharding import PartitionSpec as P

HD = 128
MESH = pl.DeviceIdType.MESH
LOG2E = 1.4426950408889634
NEG = -1e30


def kernel(
    n, sections, reach, heads_kv, group,
    q_ref, do_ref, kv_ref, docs_ref,
    dq_ref, out_ref,
    docs, qbuf, dobuf, kvbuf, bias, pbuf, dsbuf, acc, sbuf, rbuf, dqbuf,
    docsem, lsem, qsend, qrecv, kvsend, kvrecv, relsend, gsend, grecv, dqsend, dqrecv, dqloc,
):
    me = lax.axis_index("ctx")
    sec = lax.axis_index("section")
    rows = kv_ref.shape[1]
    layers = q_ref.shape[0] // rows
    core = lax.rem(me, 2)
    other = 1 - core
    chip = me // 2
    chips = n // 2
    depth = reach // 2
    place = lax.rem(chip, depth)
    blocks = reach + 2
    heads = heads_kv // 2
    gw = group * HD
    window = (reach + 1) * rows
    piece = rows // sections
    scale = HD ** (-0.5)

    def dev(ctx, section):
        return {"ctx": ctx, "section": section}

    def cols(head, width):
        return pl.ds(pl.multiple_of(head * width, HD), width)

    def local_copies(h):
        g = core * heads + h
        return [
            pltpu.make_async_copy(q_ref.at[:, cols(g, gw)], qbuf.at[h, core], lsem.at[h, 0]),
            pltpu.make_async_copy(do_ref.at[:, cols(g, gw)], dobuf.at[h, core], lsem.at[h, 1]),
            pltpu.make_async_copy(
                kv_ref.at[:, :, cols(g, HD)], kvbuf.at[h, :, reach + core], lsem.at[h, 2]
            ),
        ]

    def q_copies(h):
        g = other * heads + h
        partner = dev(2 * chip + other, sec)
        return [
            pltpu.make_async_remote_copy(
                src_ref=src.at[:, cols(g, gw)], dst_ref=dst.at[h, core],
                send_sem=qsend.at[h, k], recv_sem=qrecv.at[h, k],
                device_id=partner, device_id_type=MESH,
            )
            for k, (src, dst) in enumerate([(q_ref, qbuf), (do_ref, dobuf)])
        ]

    def kv_copy(h, d, w):
        to = lax.rem(core + w, 2)
        slot = core - 2 * d + reach
        return pltpu.make_async_remote_copy(
            src_ref=kv_ref.at[:, :, cols(to * heads + h, HD)], dst_ref=kvbuf.at[h, :, slot],
            send_sem=kvsend.at[h, d, w], recv_sem=kvrecv.at[h, slot],
            device_id=dev(2 * (chip + d) + to, sec), device_id_type=MESH,
        )

    def kv_wait(h, slot):
        return pltpu.make_async_remote_copy(
            src_ref=kv_ref.at[:, :, pl.ds(0, HD)], dst_ref=kvbuf.at[h, :, slot],
            send_sem=kvsend.at[h, 0, 0], recv_sem=kvrecv.at[h, slot],
            device_id=dev(2 * chip + other, sec), device_id_type=MESH,
        )

    def relay_copy(h, step, w):
        slot = 2 * step + w
        return pltpu.make_async_remote_copy(
            src_ref=kvbuf.at[h, :, w], dst_ref=kvbuf.at[h, :, slot],
            send_sem=relsend.at[h, step - 1, w], recv_sem=kvrecv.at[h, slot],
            device_id=dev(2 * (chip - step) + core, sec), device_id_type=MESH,
        )

    def direct(d):
        return (chip + d < chips) & (place + d < depth) if d < depth else chip + d < chips

    def relays(step):
        return (place >= step) & (chip >= depth)

    def relay(h):
        for w in range(2):
            @pl.when(chip >= depth)
            def _():
                kv_wait(h, w).wait_recv()
            for step in range(1, depth):
                pl.when(relays(step))(lambda: relay_copy(h, step, w).start())

    def g_copy(h, slot, t):
        d = (reach + 1 - slot) // 2
        owner_core = (slot - reach) % 2
        to = lax.rem(sec + t, sections)
        return pltpu.make_async_remote_copy(
            src_ref=sbuf.at[h, slot, :, pl.ds(pl.multiple_of(to * piece, piece), piece)],
            dst_ref=rbuf.at[d, sec, core, h],
            send_sem=gsend.at[h, slot, t], recv_sem=grecv.at[d, sec, core, h],
            device_id=dev(2 * (chip - d) + owner_core, to), device_id_type=MESH,
        )

    def g_wait(h, d, s, c):
        return pltpu.make_async_remote_copy(
            src_ref=sbuf.at[h, 0, :, pl.ds(0, piece)], dst_ref=rbuf.at[d, s, c, h],
            send_sem=gsend.at[h, 0, 0], recv_sem=grecv.at[d, s, c, h],
            device_id=dev(2 * chip + other, sec), device_id_type=MESH,
        )

    def dq_copy(h):
        return pltpu.make_async_remote_copy(
            src_ref=dqbuf.at[h, other], dst_ref=dq_ref.at[:, cols(core * heads + h, gw)],
            send_sem=dqsend.at[h], recv_sem=dqrecv.at[h],
            device_id=dev(2 * chip + other, sec), device_id_type=MESH,
        )

    def dq_wait(h):
        return pltpu.make_async_remote_copy(
            src_ref=dqbuf.at[h, other], dst_ref=dq_ref.at[:, cols(other * heads + h, gw)],
            send_sem=dqsend.at[h], recv_sem=dqrecv.at[h],
            device_id=dev(2 * chip + other, sec), device_id_type=MESH,
        )

    def dq_local(h):
        return pltpu.make_async_copy(
            dqbuf.at[h, core], dq_ref.at[:, cols(core * heads + h, gw)], dqloc.at[h]
        )

    barrier = pltpu.get_barrier_semaphore()
    for step in range(-depth, depth + 1):
        @pl.when((chip + step >= 0) & (chip + step < chips))
        def _():
            for w in range(2):
                for t in range(sections):
                    if step == 0 and w == 0 and t == 0:
                        continue
                    pl.semaphore_signal(
                        barrier, inc=1,
                        device_id=dev(2 * (chip + step) + lax.rem(core + w, 2), lax.rem(sec + t, sections)),
                        device_id_type=MESH,
                    )

    docs_copy = pltpu.make_async_copy(docs_ref, docs, docsem)
    docs_copy.start()
    for h in range(heads):
        for copy in local_copies(h):
            copy.start()

    near = jnp.minimum(chip, depth) + jnp.minimum(chips - 1 - chip, depth) + 1
    pl.semaphore_wait(barrier, near * (2 * sections) - 1)

    for h in range(heads):
        for d in range(depth, 0, -1):
            @pl.when(direct(d))
            def _():
                for w in range(2):
                    kv_copy(h, d, w).start()
        kv_copy(h, 0, 1).start()
        for copy in q_copies(h):
            copy.start()

    for d in range(1, depth + 1):
        @pl.when(chip - d < 0)
        def _():
            for slot in (reach - 2 * d, reach - 2 * d + 1):
                for h in range(heads):
                    kvbuf[h, :, slot] = jnp.zeros((2, rows, HD), jnp.bfloat16)

        @pl.when(chip + d >= chips)
        def _():
            rbuf[d] = jnp.zeros(rbuf.shape[1:], jnp.bfloat16)

    docs_copy.wait()
    row_at = lax.broadcasted_iota(jnp.int32, (rows, rows), 0)
    col_at = lax.broadcasted_iota(jnp.int32, (rows, rows), 1)
    for slot in range(blocks):
        at = 2 * chip - reach + slot
        kdoc = docs[pl.ds(jnp.maximum(at, 0), 1), :].astype(jnp.float32)
        kdoc = jnp.transpose(jnp.broadcast_to(kdoc, (rows, rows)))
        for sub in range(2):
            if not 0 <= slot - sub <= reach:
                continue
            qdoc = docs[pl.ds(2 * chip + sub, 1), :].astype(jnp.float32)
            kplace = at * rows + row_at
            qplace = (2 * chip + sub) * rows + col_at
            seen = (kplace <= qplace) & (kplace >= 0) & (kdoc == qdoc)
            bias[sub, (slot - sub) * rows : (slot - sub + 1) * rows] = jnp.where(seen, 0.0, NEG)

    def score_part(h, sub):
        k = kvbuf[h, 0, pl.ds(sub, reach + 1)].reshape(window, HD)
        v = kvbuf[h, 1, pl.ds(sub, reach + 1)].reshape(window, HD)
        nt = (((1,), (1,)), ((), ()))
        for i in range(group):
            at = slice(i * HD, (i + 1) * HD)
            s = lax.dot_general(k, qbuf[h, sub, :, at], nt, preferred_element_type=jnp.float32)
            dp = lax.dot_general(v, dobuf[h, sub, :, at], nt, preferred_element_type=jnp.float32)
            s = s * (scale * LOG2E) + jnp.concatenate([bias[sub]] * layers, axis=1)
            e = jnp.exp2(s - jnp.max(s, axis=0, keepdims=True))
            inverse = 1.0 / jnp.sum(e, axis=0, keepdims=True)
            delta = jnp.sum(e * dp, axis=0, keepdims=True) * inverse
            p = (e * inverse).astype(jnp.bfloat16)
            to = slice(i * layers * rows, (i + 1) * layers * rows)
            pbuf[:, to] = p
            dsbuf[:, to] = (p.astype(jnp.float32) * (dp - delta)).astype(jnp.bfloat16)

    def key_part(h, sub):
        keys_at = pl.ds(pl.multiple_of(sub * rows, rows), window)
        for k, (weights, buf) in enumerate([(dsbuf, qbuf), (pbuf, dobuf)]):
            stack = jnp.concatenate(
                [buf[h, sub, :, i * HD : (i + 1) * HD] for i in range(group)], axis=0
            )
            acc[k, keys_at] += jnp.dot(weights[...], stack, preferred_element_type=jnp.float32)

    def query_part(h, sub):
        kt = jnp.transpose(kvbuf[h, 0, pl.ds(sub, reach + 1)].reshape(window, HD))
        dqt = jnp.dot(kt, dsbuf[...], preferred_element_type=jnp.float32) * scale
        for i in range(group):
            dqbuf[h, sub, :, i * HD : (i + 1) * HD] = jnp.transpose(
                dqt[:, i * layers * rows : (i + 1) * layers * rows]
            ).astype(jnp.bfloat16)

    relay(0)

    def head_step(h, unused):
        local_copies(h)[2].wait()
        for slot in range(2, blocks):
            at = 2 * chip - reach + slot
            if slot < reach:
                condition = at >= 0
            else:
                condition = core != slot - reach

            @pl.when(condition)
            def _():
                kv_wait(h, slot).wait_recv()

        acc[...] = jnp.zeros_like(acc)
        for copy in local_copies(h)[:2]:
            copy.wait()
        score_part(h, core)
        key_part(h, core)
        query_part(h, core)
        dq_local(h).start()

        @pl.when(h + 1 < heads)
        def _():
            relay(h + 1)

        for copy in q_copies(h):
            copy.wait_recv()
        score_part(h, other)
        key_part(h, other)
        for slot in range(blocks):
            at = slice(slot * rows, (slot + 1) * rows)
            sbuf[h, slot, 0] = (acc[0, at] * scale).astype(jnp.bfloat16)
            sbuf[h, slot, 1] = acc[1, at].astype(jnp.bfloat16)
        own = pl.ds(pl.multiple_of(sec * piece, piece), piece)
        rbuf[0, sec, core, h] = sbuf[h, reach + core, :, own]
        for slot in range(blocks):
            for t in range(sections):
                if slot < reach:
                    condition = 2 * chip - reach + slot >= 0
                elif t == 0:
                    condition = core != slot - reach
                else:
                    condition = None
                if condition is None:
                    g_copy(h, slot, t).start()
                else:
                    pl.when(condition)(lambda: g_copy(h, slot, t).start())
        query_part(h, other)
        dq_copy(h).start()
        return unused

    lax.fori_loop(0, heads, head_step, 0)

    for h in range(heads):
        for d in range(depth + 1):
            for s in range(sections):
                for c in range(2):
                    if d == 0:
                        condition = (sec != s) | (core != c)
                    else:
                        condition = chip + d < chips

                    @pl.when(condition)
                    def _():
                        g_wait(h, d, s, c).wait_recv()
    for c in range(2):
        for h in range(heads):
            total = None
            for d in range(depth + 1):
                for s in range(sections):
                    term = rbuf[d, s, c, h].astype(jnp.float32)
                    total = term if total is None else total + term
            g = c * heads + h
            out_ref[:, :, g * HD : (g + 1) * HD] = total.astype(jnp.bfloat16)

    def finish(h, unused):
        dq_wait(h).wait_recv()
        dq_copy(h).wait_send()
        dq_local(h).wait()
        for copy in q_copies(h):
            copy.wait_send()
        kv_copy(h, 0, 1).wait_send()
        for d in range(1, depth + 1):
            @pl.when(direct(d))
            def _():
                for w in range(2):
                    kv_copy(h, d, w).wait_send()
        for step in range(1, depth):
            for w in range(2):
                pl.when(relays(step))(lambda: relay_copy(h, step, w).wait_send())
        for slot in range(blocks):
            for t in range(sections):
                if slot < reach:
                    condition = 2 * chip - reach + slot >= 0
                elif t == 0:
                    condition = core != slot - reach
                else:
                    condition = None
                if condition is None:
                    g_copy(h, slot, t).wait_send()
                else:
                    pl.when(condition)(lambda: g_copy(h, slot, t).wait_send())
        return unused

    lax.fori_loop(0, heads, finish, 0)


def body(queries, grad_out, keys_values, doc_ids):
    layers, rows, width = queries.shape
    kv_width = keys_values.shape[2]
    heads_kv = kv_width // HD
    group = width // kv_width
    n = lax.axis_size("ctx")
    sections = lax.axis_size("section")
    reach = n // 4
    heads = heads_kv // 2
    blocks = reach + 2
    window = (reach + 1) * rows
    piece = rows // sections
    depth = reach // 2
    bf, f32 = jnp.bfloat16, jnp.float32
    dma = pltpu.SemaphoreType.DMA
    hbm = pl.BlockSpec(memory_space=pl.ANY)
    vmem = pl.BlockSpec(memory_space=pltpu.VMEM)
    grad_queries, grad_kv = pl.pallas_call(
        functools.partial(kernel, n, sections, reach, heads_kv, group),
        out_shape=(
            jax.ShapeDtypeStruct((layers * rows, width), bf),
            jax.ShapeDtypeStruct((2, piece, kv_width), bf),
        ),
        in_specs=[hbm, hbm, hbm, hbm],
        out_specs=(hbm, vmem),
        scratch_shapes=[
            pltpu.VMEM((n, rows), jnp.int32),
            pltpu.VMEM((heads, 2, layers * rows, group * HD), bf),
            pltpu.VMEM((heads, 2, layers * rows, group * HD), bf),
            pltpu.VMEM((heads, 2, blocks, rows, HD), bf),
            pltpu.VMEM((2, window, rows), f32),
            pltpu.VMEM((window, group * layers * rows), bf),
            pltpu.VMEM((window, group * layers * rows), bf),
            pltpu.VMEM((2, blocks * rows, HD), f32),
            pltpu.VMEM((heads, blocks, 2, rows, HD), bf),
            pltpu.VMEM((depth + 1, sections, 2, heads, 2, piece, HD), bf),
            pltpu.VMEM((heads, 2, layers * rows, group * HD), bf),
            dma,
            dma((heads, 3)),
            dma((heads, 2)),
            dma((heads, 2)),
            dma((heads, depth + 1, 2)),
            dma((heads, blocks)),
            dma((heads, max(depth - 1, 1), 2)),
            dma((heads, blocks, sections)),
            dma((depth + 1, sections, 2, heads)),
            dma((heads,)),
            dma((heads,)),
            dma((heads,)),
        ],
        compiler_params=pltpu.CompilerParams(
            collective_id=0, has_side_effects=True, vmem_limit_bytes=67043328
        ),
        name="cross_backward",
    )(
        queries.reshape(layers * rows, width), grad_out.reshape(layers * rows, width),
        keys_values, doc_ids.reshape(n, rows),
    )
    return grad_queries.reshape(queries.shape), grad_kv


def solution(mesh):
    return jax.shard_map(
        body,
        mesh=mesh,
        in_specs=(P("section", "ctx", None), P("section", "ctx", None), P(None, "ctx", None), P()),
        out_specs=(P("section", "ctx", None), P(None, ("ctx", "section"), None)),
        check_vma=False,
    )
```

```python
import functools

import jax
import jax.numpy as jnp
from jax import lax
from jax.experimental import pallas as pl
from jax.experimental.pallas import tpu as pltpu
from jax.sharding import PartitionSpec as P

HD = 128
MESH = pl.DeviceIdType.MESH
LOG2E = 1.4426950408889634
NEG = -1e30


def kernel(
    n, sections, reach, heads_kv, group,
    q_ref, do_ref, kv_ref, docs_ref,
    dq_ref, out_ref,
    docs, qbuf, dobuf, kvbuf, bias, pbuf, dsbuf, acc, sbuf, rbuf, dqbuf,
    docsem, lsem, qsend, qrecv, kvsend, kvrecv, relsend, gsend, grecv, dqsend, dqrecv, dqloc,
):
    me = lax.axis_index("ctx")
    sec = lax.axis_index("section")
    rows = kv_ref.shape[1]
    layers = q_ref.shape[0] // rows
    core = lax.rem(me, 2)
    other = 1 - core
    chip = me // 2
    chips = n // 2
    depth = reach // 2
    place = lax.rem(chip, depth)
    blocks = reach + 2
    heads = heads_kv // 2
    gw = group * HD
    window = (reach + 1) * rows
    piece = rows // sections
    scale = HD ** (-0.5)

    def dev(ctx, section):
        return {"ctx": ctx, "section": section}

    def cols(head, width):
        return pl.ds(pl.multiple_of(head * width, HD), width)

    def local_copies(h):
        g = core * heads + h
        return [
            pltpu.make_async_copy(q_ref.at[:, cols(g, gw)], qbuf.at[h, core], lsem.at[h, 0]),
            pltpu.make_async_copy(do_ref.at[:, cols(g, gw)], dobuf.at[h, core], lsem.at[h, 1]),
            pltpu.make_async_copy(
                kv_ref.at[:, :, cols(g, HD)], kvbuf.at[h, :, reach + core], lsem.at[h, 2]
            ),
        ]

    def q_copies(h):
        g = other * heads + h
        partner = dev(2 * chip + other, sec)
        return [
            pltpu.make_async_remote_copy(
                src_ref=src.at[:, cols(g, gw)], dst_ref=dst.at[h, core],
                send_sem=qsend.at[h, k], recv_sem=qrecv.at[h, k],
                device_id=partner, device_id_type=MESH,
            )
            for k, (src, dst) in enumerate([(q_ref, qbuf), (do_ref, dobuf)])
        ]

    def kv_copy(h, d, w):
        to = lax.rem(core + w, 2)
        slot = core - 2 * d + reach
        return pltpu.make_async_remote_copy(
            src_ref=kv_ref.at[:, :, cols(to * heads + h, HD)], dst_ref=kvbuf.at[h, :, slot],
            send_sem=kvsend.at[h, d, w], recv_sem=kvrecv.at[h, slot],
            device_id=dev(2 * (chip + d) + to, sec), device_id_type=MESH,
        )

    def kv_wait(h, slot):
        return pltpu.make_async_remote_copy(
            src_ref=kv_ref.at[:, :, pl.ds(0, HD)], dst_ref=kvbuf.at[h, :, slot],
            send_sem=kvsend.at[h, 0, 0], recv_sem=kvrecv.at[h, slot],
            device_id=dev(2 * chip + other, sec), device_id_type=MESH,
        )

    def relay_copy(h, step, w):
        slot = 2 * step + w
        return pltpu.make_async_remote_copy(
            src_ref=kvbuf.at[h, :, w], dst_ref=kvbuf.at[h, :, slot],
            send_sem=relsend.at[h, step - 1, w], recv_sem=kvrecv.at[h, slot],
            device_id=dev(2 * (chip - step) + core, sec), device_id_type=MESH,
        )

    def direct(d):
        return (chip + d < chips) & (place + d < depth) if d < depth else chip + d < chips

    def relays(step):
        return (place >= step) & (chip >= depth)

    def relay(h):
        for w in range(2):
            @pl.when(chip >= depth)
            def _():
                kv_wait(h, w).wait_recv()
            for step in range(1, depth):
                pl.when(relays(step))(lambda: relay_copy(h, step, w).start())

    def g_copy(h, slot, t):
        d = (reach + 1 - slot) // 2
        owner_core = (slot - reach) % 2
        to = lax.rem(sec + t, sections)
        return pltpu.make_async_remote_copy(
            src_ref=sbuf.at[h, slot, :, pl.ds(pl.multiple_of(to * piece, piece), piece)],
            dst_ref=rbuf.at[d, sec, core, h],
            send_sem=gsend.at[h, slot, t], recv_sem=grecv.at[d, sec, core, h],
            device_id=dev(2 * (chip - d) + owner_core, to), device_id_type=MESH,
        )

    def g_wait(h, d, s, c):
        return pltpu.make_async_remote_copy(
            src_ref=sbuf.at[h, 0, :, pl.ds(0, piece)], dst_ref=rbuf.at[d, s, c, h],
            send_sem=gsend.at[h, 0, 0], recv_sem=grecv.at[d, s, c, h],
            device_id=dev(2 * chip + other, sec), device_id_type=MESH,
        )

    def dq_copy(h):
        return pltpu.make_async_remote_copy(
            src_ref=dqbuf.at[h, other], dst_ref=dq_ref.at[:, cols(core * heads + h, gw)],
            send_sem=dqsend.at[h], recv_sem=dqrecv.at[h],
            device_id=dev(2 * chip + other, sec), device_id_type=MESH,
        )

    def dq_wait(h):
        return pltpu.make_async_remote_copy(
            src_ref=dqbuf.at[h, other], dst_ref=dq_ref.at[:, cols(other * heads + h, gw)],
            send_sem=dqsend.at[h], recv_sem=dqrecv.at[h],
            device_id=dev(2 * chip + other, sec), device_id_type=MESH,
        )

    def dq_local(h):
        return pltpu.make_async_copy(
            dqbuf.at[h, core], dq_ref.at[:, cols(core * heads + h, gw)], dqloc.at[h]
        )

    barrier = pltpu.get_barrier_semaphore()

    def greet(ctx, section):
        pl.semaphore_signal(barrier, inc=1, device_id=dev(ctx, section), device_id_type=MESH)

    for step in range(-depth, depth + 1):
        if abs(step) == depth:
            condition = (chip + step >= 0) & (chip + step < chips)
        else:
            condition = (place + step >= 0) & (place + step < depth)

        @pl.when(condition)
        def _():
            for w in range(2):
                if step == 0 and w == 0:
                    continue
                greet(2 * (chip + step) + lax.rem(core + w, 2), sec)

    for w in range(2):
        for t in range(1, sections):
            greet(2 * chip + lax.rem(core + w, 2), lax.rem(sec + t, sections))

    docs_copy = pltpu.make_async_copy(docs_ref, docs, docsem)
    docs_copy.start()
    for h in range(heads):
        for copy in local_copies(h):
            copy.start()

    near = depth + (chip >= depth).astype(jnp.int32) + (chip + depth < chips).astype(jnp.int32)
    pl.semaphore_wait(barrier, 2 * near - 1 + 2 * (sections - 1))

    for h in range(heads):
        for d in range(depth, 0, -1):
            @pl.when(direct(d))
            def _():
                for w in range(2):
                    kv_copy(h, d, w).start()
        kv_copy(h, 0, 1).start()
        for copy in q_copies(h):
            copy.start()

    for d in range(1, depth + 1):
        @pl.when(chip - d < 0)
        def _():
            for slot in (reach - 2 * d, reach - 2 * d + 1):
                for h in range(heads):
                    kvbuf[h, :, slot] = jnp.zeros((2, rows, HD), jnp.bfloat16)

        @pl.when(chip + d >= chips)
        def _():
            rbuf[d] = jnp.zeros(rbuf.shape[1:], jnp.bfloat16)

    docs_copy.wait()
    row_at = lax.broadcasted_iota(jnp.int32, (rows, rows), 0)
    col_at = lax.broadcasted_iota(jnp.int32, (rows, rows), 1)
    for slot in range(blocks):
        at = 2 * chip - reach + slot
        kdoc = docs[pl.ds(jnp.maximum(at, 0), 1), :].astype(jnp.float32)
        kdoc = jnp.transpose(jnp.broadcast_to(kdoc, (rows, rows)))
        for sub in range(2):
            if not 0 <= slot - sub <= reach:
                continue
            qdoc = docs[pl.ds(2 * chip + sub, 1), :].astype(jnp.float32)
            kplace = at * rows + row_at
            qplace = (2 * chip + sub) * rows + col_at
            seen = (kplace <= qplace) & (kplace >= 0) & (kdoc == qdoc)
            bias[sub, (slot - sub) * rows : (slot - sub + 1) * rows] = jnp.where(seen, 0.0, NEG)

    def score_part(h, sub):
        k = kvbuf[h, 0, pl.ds(sub, reach + 1)].reshape(window, HD)
        v = kvbuf[h, 1, pl.ds(sub, reach + 1)].reshape(window, HD)
        nt = (((1,), (1,)), ((), ()))
        for i in range(group):
            at = slice(i * HD, (i + 1) * HD)
            s = lax.dot_general(k, qbuf[h, sub, :, at], nt, preferred_element_type=jnp.float32)
            dp = lax.dot_general(v, dobuf[h, sub, :, at], nt, preferred_element_type=jnp.float32)
            s = s * (scale * LOG2E) + jnp.concatenate([bias[sub]] * layers, axis=1)
            e = jnp.exp2(s - jnp.max(s, axis=0, keepdims=True))
            inverse = 1.0 / jnp.sum(e, axis=0, keepdims=True)
            delta = jnp.sum(e * dp, axis=0, keepdims=True) * inverse
            p = (e * inverse).astype(jnp.bfloat16)
            to = slice(i * layers * rows, (i + 1) * layers * rows)
            pbuf[:, to] = p
            dsbuf[h, sub, :, to] = (p.astype(jnp.float32) * (dp - delta)).astype(jnp.bfloat16)

    def key_part(h, sub):
        keys_at = pl.ds(pl.multiple_of(sub * rows, rows), window)
        for k, (weights, buf) in enumerate([(dsbuf.at[h, sub], qbuf), (pbuf, dobuf)]):
            stack = jnp.concatenate(
                [buf[h, sub, :, i * HD : (i + 1) * HD] for i in range(group)], axis=0
            )
            acc[k, keys_at] += jnp.dot(weights[...], stack, preferred_element_type=jnp.float32)

    def query_part(h, sub):
        kt = jnp.transpose(kvbuf[h, 0, pl.ds(sub, reach + 1)].reshape(window, HD))
        dqt = jnp.dot(kt, dsbuf[h, sub], preferred_element_type=jnp.float32) * scale
        for i in range(group):
            dqbuf[h, sub, :, i * HD : (i + 1) * HD] = jnp.transpose(
                dqt[:, i * layers * rows : (i + 1) * layers * rows]
            ).astype(jnp.bfloat16)

    relay(0)

    def head_step(h, unused):
        local_copies(h)[2].wait()
        for slot in range(2, blocks):
            at = 2 * chip - reach + slot
            if slot < reach:
                condition = at >= 0
            else:
                condition = core != slot - reach

            @pl.when(condition)
            def _():
                kv_wait(h, slot).wait_recv()

        acc[...] = jnp.zeros_like(acc)
        for copy in local_copies(h)[:2]:
            copy.wait()
        score_part(h, core)
        key_part(h, core)

        @pl.when(h + 1 < heads)
        def _():
            relay(h + 1)

        for copy in q_copies(h):
            copy.wait_recv()
        score_part(h, other)
        key_part(h, other)
        for slot in range(blocks):
            at = slice(slot * rows, (slot + 1) * rows)
            sbuf[h, slot, 0] = (acc[0, at] * scale).astype(jnp.bfloat16)
            sbuf[h, slot, 1] = acc[1, at].astype(jnp.bfloat16)
        own = pl.ds(pl.multiple_of(sec * piece, piece), piece)
        rbuf[0, sec, core, h] = sbuf[h, reach + core, :, own]
        for slot in range(blocks):
            for t in range(sections):
                if slot < reach:
                    condition = 2 * chip - reach + slot >= 0
                elif t == 0:
                    condition = core != slot - reach
                else:
                    condition = None
                if condition is None:
                    g_copy(h, slot, t).start()
                else:
                    pl.when(condition)(lambda: g_copy(h, slot, t).start())
        return unused

    lax.fori_loop(0, heads, head_step, 0)

    def query_step(h, unused):
        query_part(h, other)
        dq_copy(h).start()
        query_part(h, core)
        dq_local(h).start()
        return unused

    lax.fori_loop(0, heads, query_step, 0)

    for h in range(heads):
        for d in range(depth + 1):
            for s in range(sections):
                for c in range(2):
                    if d == 0:
                        condition = (sec != s) | (core != c)
                    else:
                        condition = chip + d < chips

                    @pl.when(condition)
                    def _():
                        g_wait(h, d, s, c).wait_recv()
    for c in range(2):
        for h in range(heads):
            total = None
            for d in range(depth + 1):
                for s in range(sections):
                    term = rbuf[d, s, c, h].astype(jnp.float32)
                    total = term if total is None else total + term
            g = c * heads + h
            out_ref[:, :, g * HD : (g + 1) * HD] = total.astype(jnp.bfloat16)

    def finish(h, unused):
        dq_wait(h).wait_recv()
        dq_copy(h).wait_send()
        dq_local(h).wait()
        for copy in q_copies(h):
            copy.wait_send()
        kv_copy(h, 0, 1).wait_send()
        for d in range(1, depth + 1):
            @pl.when(direct(d))
            def _():
                for w in range(2):
                    kv_copy(h, d, w).wait_send()
        for step in range(1, depth):
            for w in range(2):
                pl.when(relays(step))(lambda: relay_copy(h, step, w).wait_send())
        for slot in range(blocks):
            for t in range(sections):
                if slot < reach:
                    condition = 2 * chip - reach + slot >= 0
                elif t == 0:
                    condition = core != slot - reach
                else:
                    condition = None
                if condition is None:
                    g_copy(h, slot, t).wait_send()
                else:
                    pl.when(condition)(lambda: g_copy(h, slot, t).wait_send())
        return unused

    lax.fori_loop(0, heads, finish, 0)


def body(queries, grad_out, keys_values, doc_ids):
    layers, rows, width = queries.shape
    kv_width = keys_values.shape[2]
    heads_kv = kv_width // HD
    group = width // kv_width
    n = lax.axis_size("ctx")
    sections = lax.axis_size("section")
    reach = n // 4
    heads = heads_kv // 2
    blocks = reach + 2
    window = (reach + 1) * rows
    piece = rows // sections
    depth = reach // 2
    bf, f32 = jnp.bfloat16, jnp.float32
    dma = pltpu.SemaphoreType.DMA
    hbm = pl.BlockSpec(memory_space=pl.ANY)
    vmem = pl.BlockSpec(memory_space=pltpu.VMEM)
    grad_queries, grad_kv = pl.pallas_call(
        functools.partial(kernel, n, sections, reach, heads_kv, group),
        out_shape=(
            jax.ShapeDtypeStruct((layers * rows, width), bf),
            jax.ShapeDtypeStruct((2, piece, kv_width), bf),
        ),
        in_specs=[hbm, hbm, hbm, hbm],
        out_specs=(hbm, vmem),
        scratch_shapes=[
            pltpu.VMEM((n, rows), jnp.int32),
            pltpu.VMEM((heads, 2, layers * rows, group * HD), bf),
            pltpu.VMEM((heads, 2, layers * rows, group * HD), bf),
            pltpu.VMEM((heads, 2, blocks, rows, HD), bf),
            pltpu.VMEM((2, window, rows), f32),
            pltpu.VMEM((window, group * layers * rows), bf),
            pltpu.VMEM((heads, 2, window, group * layers * rows), bf),
            pltpu.VMEM((2, blocks * rows, HD), f32),
            pltpu.VMEM((heads, blocks, 2, rows, HD), bf),
            pltpu.VMEM((depth + 1, sections, 2, heads, 2, piece, HD), bf),
            pltpu.VMEM((heads, 2, layers * rows, group * HD), bf),
            dma,
            dma((heads, 3)),
            dma((heads, 2)),
            dma((heads, 2)),
            dma((heads, depth + 1, 2)),
            dma((heads, blocks)),
            dma((heads, max(depth - 1, 1), 2)),
            dma((heads, blocks, sections)),
            dma((depth + 1, sections, 2, heads)),
            dma((heads,)),
            dma((heads,)),
            dma((heads,)),
        ],
        compiler_params=pltpu.CompilerParams(
            collective_id=0, has_side_effects=True, vmem_limit_bytes=67043328
        ),
        name="cross_backward",
    )(
        queries.reshape(layers * rows, width), grad_out.reshape(layers * rows, width),
        keys_values, doc_ids.reshape(n, rows),
    )
    return grad_queries.reshape(queries.shape), grad_kv


def solution(mesh):
    return jax.shard_map(
        body,
        mesh=mesh,
        in_specs=(P("section", "ctx", None), P("section", "ctx", None), P(None, "ctx", None), P()),
        out_specs=(P("section", "ctx", None), P(None, ("ctx", "section"), None)),
        check_vma=False,
    )
```

```python
import functools

import jax
import jax.numpy as jnp
from jax import lax
from jax.experimental import pallas as pl
from jax.experimental.pallas import tpu as pltpu
from jax.sharding import PartitionSpec as P

HD = 128
MESH = pl.DeviceIdType.MESH
LOG2E = 1.4426950408889634
NEG = -1e30


def kernel(
    n, sections, reach, heads_kv, group,
    q_ref, do_ref, kv_ref, docs_ref,
    dq_ref, out_ref,
    docs, qbuf, dobuf, kvbuf, bias, pbuf, dsbuf, acc, sbuf, xbuf, tbuf, rbuf, dqbuf,
    docsem, lsem, qsend, qrecv, kvsend, kvrecv, relsend, xsend, xrecv, gsend, grecv, dqsend, dqrecv, dqloc,
):
    me = lax.axis_index("ctx")
    sec = lax.axis_index("section")
    rows = kv_ref.shape[1]
    layers = q_ref.shape[0] // rows
    core = lax.rem(me, 2)
    other = 1 - core
    chip = me // 2
    chips = n // 2
    depth = reach // 2
    place = lax.rem(chip, depth)
    blocks = reach + 2
    heads = heads_kv // 2
    gw = group * HD
    window = (reach + 1) * rows
    piece = rows // sections
    scale = HD ** (-0.5)

    def dev(ctx, section):
        return {"ctx": ctx, "section": section}

    def cols(head, width):
        return pl.ds(pl.multiple_of(head * width, HD), width)

    def local_copies(h):
        g = core * heads + h
        return [
            pltpu.make_async_copy(q_ref.at[:, cols(g, gw)], qbuf.at[h, core], lsem.at[h, 0]),
            pltpu.make_async_copy(do_ref.at[:, cols(g, gw)], dobuf.at[h, core], lsem.at[h, 1]),
            pltpu.make_async_copy(
                kv_ref.at[:, :, cols(g, HD)], kvbuf.at[h, :, reach + core], lsem.at[h, 2]
            ),
        ]

    def q_copies(h):
        g = other * heads + h
        partner = dev(2 * chip + other, sec)
        return [
            pltpu.make_async_remote_copy(
                src_ref=src.at[:, cols(g, gw)], dst_ref=dst.at[h, core],
                send_sem=qsend.at[h, k], recv_sem=qrecv.at[h, k],
                device_id=partner, device_id_type=MESH,
            )
            for k, (src, dst) in enumerate([(q_ref, qbuf), (do_ref, dobuf)])
        ]

    def kv_copy(h, d, w):
        to = lax.rem(core + w, 2)
        slot = core - 2 * d + reach
        return pltpu.make_async_remote_copy(
            src_ref=kv_ref.at[:, :, cols(to * heads + h, HD)], dst_ref=kvbuf.at[h, :, slot],
            send_sem=kvsend.at[h, d, w], recv_sem=kvrecv.at[h, slot],
            device_id=dev(2 * (chip + d) + to, sec), device_id_type=MESH,
        )

    def kv_wait(h, slot):
        return pltpu.make_async_remote_copy(
            src_ref=kv_ref.at[:, :, pl.ds(0, HD)], dst_ref=kvbuf.at[h, :, slot],
            send_sem=kvsend.at[h, 0, 0], recv_sem=kvrecv.at[h, slot],
            device_id=dev(2 * chip + other, sec), device_id_type=MESH,
        )

    def relay_copy(h, step, w):
        slot = 2 * step + w
        return pltpu.make_async_remote_copy(
            src_ref=kvbuf.at[h, :, w], dst_ref=kvbuf.at[h, :, slot],
            send_sem=relsend.at[h, step - 1, w], recv_sem=kvrecv.at[h, slot],
            device_id=dev(2 * (chip - step) + core, sec), device_id_type=MESH,
        )

    def direct(d):
        return (chip + d < chips) & (place + d < depth) if d < depth else chip + d < chips

    def relays(step):
        return (place >= step) & (chip >= depth)

    def relay(h):
        for w in range(2):
            @pl.when(chip >= depth)
            def _():
                kv_wait(h, w).wait_recv()
            for step in range(1, depth):
                pl.when(relays(step))(lambda: relay_copy(h, step, w).start())

    def x_copy(h, slot, t):
        to = lax.rem(sec + t, sections)
        return pltpu.make_async_remote_copy(
            src_ref=sbuf.at[h, slot, :, pl.ds(pl.multiple_of(to * piece, piece), piece)],
            dst_ref=xbuf.at[h, slot, t - 1],
            send_sem=xsend.at[h, slot, t - 1], recv_sem=xrecv.at[h, slot, t - 1],
            device_id=dev(me, to), device_id_type=MESH,
        )

    def g_copy(h, slot):
        d = (reach + 1 - slot) // 2
        return pltpu.make_async_remote_copy(
            src_ref=tbuf.at[h, slot], dst_ref=rbuf.at[d, core, h],
            send_sem=gsend.at[h, slot], recv_sem=grecv.at[d, core, h],
            device_id=dev(2 * (chip - d) + (slot - reach) % 2, sec), device_id_type=MESH,
        )

    def g_wait(h, d, c):
        return pltpu.make_async_remote_copy(
            src_ref=tbuf.at[h, 0], dst_ref=rbuf.at[d, c, h],
            send_sem=gsend.at[h, 0], recv_sem=grecv.at[d, c, h],
            device_id=dev(2 * chip + other, sec), device_id_type=MESH,
        )

    def when_block(slot, run):
        if slot < reach:
            pl.when(2 * chip - reach + slot >= 0)(run)
        else:
            run()

    def when_sent(slot, run):
        pl.when(2 * chip - reach + slot >= 0 if slot < reach else core != slot - reach)(run)

    def scatter(h):
        def send(slot):
            for t in range(1, sections):
                x_copy(h, slot, t).start()

        for slot in range(blocks):
            when_block(slot, functools.partial(send, slot))

    def deliver(h):
        own = pl.ds(pl.multiple_of(sec * piece, piece), piece)

        def run(slot):
            total = sbuf[h, slot, :, own].astype(jnp.float32)
            for t in range(1, sections):
                x_copy(h, slot, t).wait_recv()
                total = total + xbuf[h, slot, t - 1].astype(jnp.float32)
            tbuf[h, slot] = total.astype(jnp.bfloat16)
            when_sent(slot, lambda: g_copy(h, slot).start())

        for slot in range(blocks):
            when_block(slot, functools.partial(run, slot))
        rbuf[0, core, h] = tbuf[h, reach + core]

    def dq_copy(h):
        return pltpu.make_async_remote_copy(
            src_ref=dqbuf.at[h, other], dst_ref=dq_ref.at[:, cols(core * heads + h, gw)],
            send_sem=dqsend.at[h], recv_sem=dqrecv.at[h],
            device_id=dev(2 * chip + other, sec), device_id_type=MESH,
        )

    def dq_wait(h):
        return pltpu.make_async_remote_copy(
            src_ref=dqbuf.at[h, other], dst_ref=dq_ref.at[:, cols(other * heads + h, gw)],
            send_sem=dqsend.at[h], recv_sem=dqrecv.at[h],
            device_id=dev(2 * chip + other, sec), device_id_type=MESH,
        )

    def dq_local(h):
        return pltpu.make_async_copy(
            dqbuf.at[h, core], dq_ref.at[:, cols(core * heads + h, gw)], dqloc.at[h]
        )

    barrier = pltpu.get_barrier_semaphore()

    def greet(ctx, section):
        pl.semaphore_signal(barrier, inc=1, device_id=dev(ctx, section), device_id_type=MESH)

    for step in range(-depth, depth + 1):
        if abs(step) == depth:
            condition = (chip + step >= 0) & (chip + step < chips)
        else:
            condition = (place + step >= 0) & (place + step < depth)

        @pl.when(condition)
        def _():
            for w in range(2):
                if step == 0 and w == 0:
                    continue
                greet(2 * (chip + step) + lax.rem(core + w, 2), sec)

    for w in range(2):
        for t in range(1, sections):
            greet(2 * chip + lax.rem(core + w, 2), lax.rem(sec + t, sections))

    docs_copy = pltpu.make_async_copy(docs_ref, docs, docsem)
    docs_copy.start()
    for h in range(heads):
        for copy in local_copies(h):
            copy.start()

    near = depth + (chip >= depth).astype(jnp.int32) + (chip + depth < chips).astype(jnp.int32)
    pl.semaphore_wait(barrier, 2 * near - 1 + 2 * (sections - 1))

    for h in range(heads):
        for d in range(depth, 0, -1):
            @pl.when(direct(d))
            def _():
                for w in range(2):
                    kv_copy(h, d, w).start()
        kv_copy(h, 0, 1).start()
        for copy in q_copies(h):
            copy.start()

    for d in range(1, depth + 1):
        @pl.when(chip - d < 0)
        def _():
            for slot in (reach - 2 * d, reach - 2 * d + 1):
                for h in range(heads):
                    kvbuf[h, :, slot] = jnp.zeros((2, rows, HD), jnp.bfloat16)

        @pl.when(chip + d >= chips)
        def _():
            rbuf[d] = jnp.zeros(rbuf.shape[1:], jnp.bfloat16)

    docs_copy.wait()
    row_at = lax.broadcasted_iota(jnp.int32, (rows, rows), 0)
    col_at = lax.broadcasted_iota(jnp.int32, (rows, rows), 1)
    for slot in range(blocks):
        at = 2 * chip - reach + slot
        kdoc = docs[pl.ds(jnp.maximum(at, 0), 1), :].astype(jnp.float32)
        kdoc = jnp.transpose(jnp.broadcast_to(kdoc, (rows, rows)))
        for sub in range(2):
            if not 0 <= slot - sub <= reach:
                continue
            qdoc = docs[pl.ds(2 * chip + sub, 1), :].astype(jnp.float32)
            kplace = at * rows + row_at
            qplace = (2 * chip + sub) * rows + col_at
            seen = (kplace <= qplace) & (kplace >= 0) & (kdoc == qdoc)
            bias[sub, (slot - sub) * rows : (slot - sub + 1) * rows] = jnp.where(seen, 0.0, NEG)

    def score_part(h, sub):
        k = kvbuf[h, 0, pl.ds(sub, reach + 1)].reshape(window, HD)
        v = kvbuf[h, 1, pl.ds(sub, reach + 1)].reshape(window, HD)
        nt = (((1,), (1,)), ((), ()))
        for i in range(group):
            at = slice(i * HD, (i + 1) * HD)
            s = lax.dot_general(k, qbuf[h, sub, :, at], nt, preferred_element_type=jnp.float32)
            dp = lax.dot_general(v, dobuf[h, sub, :, at], nt, preferred_element_type=jnp.float32)
            s = s * (scale * LOG2E) + jnp.concatenate([bias[sub]] * layers, axis=1)
            e = jnp.exp2(s - jnp.max(s, axis=0, keepdims=True))
            inverse = 1.0 / jnp.sum(e, axis=0, keepdims=True)
            delta = jnp.sum(e * dp, axis=0, keepdims=True) * inverse
            p = (e * inverse).astype(jnp.bfloat16)
            to = slice(i * layers * rows, (i + 1) * layers * rows)
            pbuf[:, to] = p
            dsbuf[h, sub, :, to] = (p.astype(jnp.float32) * (dp - delta)).astype(jnp.bfloat16)

    def key_part(h, sub):
        keys_at = pl.ds(pl.multiple_of(sub * rows, rows), window)
        for k, (weights, buf) in enumerate([(dsbuf.at[h, sub], qbuf), (pbuf, dobuf)]):
            stack = jnp.concatenate(
                [buf[h, sub, :, i * HD : (i + 1) * HD] for i in range(group)], axis=0
            )
            acc[k, keys_at] += jnp.dot(weights[...], stack, preferred_element_type=jnp.float32)

    def query_part(h, sub):
        kt = jnp.transpose(kvbuf[h, 0, pl.ds(sub, reach + 1)].reshape(window, HD))
        dqt = jnp.dot(kt, dsbuf[h, sub], preferred_element_type=jnp.float32) * scale
        for i in range(group):
            dqbuf[h, sub, :, i * HD : (i + 1) * HD] = jnp.transpose(
                dqt[:, i * layers * rows : (i + 1) * layers * rows]
            ).astype(jnp.bfloat16)

    relay(0)

    def head_step(h, unused):
        local_copies(h)[2].wait()
        for slot in range(2, blocks):
            at = 2 * chip - reach + slot
            if slot < reach:
                condition = at >= 0
            else:
                condition = core != slot - reach

            @pl.when(condition)
            def _():
                kv_wait(h, slot).wait_recv()

        acc[...] = jnp.zeros_like(acc)
        for copy in local_copies(h)[:2]:
            copy.wait()
        score_part(h, core)
        key_part(h, core)

        @pl.when(h + 1 < heads)
        def _():
            relay(h + 1)

        for copy in q_copies(h):
            copy.wait_recv()
        score_part(h, other)
        key_part(h, other)
        for slot in range(blocks):
            at = slice(slot * rows, (slot + 1) * rows)
            sbuf[h, slot, 0] = (acc[0, at] * scale).astype(jnp.bfloat16)
            sbuf[h, slot, 1] = acc[1, at].astype(jnp.bfloat16)
        scatter(h)

        @pl.when(h > 0)
        def _():
            deliver(h - 1)

        return unused

    lax.fori_loop(0, heads, head_step, 0)

    def query_step(h, unused):
        query_part(h, other)
        dq_copy(h).start()
        query_part(h, core)
        dq_local(h).start()
        return unused

    lax.fori_loop(0, heads, query_step, 0)

    deliver(heads - 1)

    for h in range(heads):
        for c in range(2):
            for d in range(depth, -1, -1):
                pl.when(core != c if d == 0 else chip + d < chips)(lambda: g_wait(h, d, c).wait_recv())
            total = rbuf[0, c, h].astype(jnp.float32)
            for d in range(1, depth + 1):
                total = total + rbuf[d, c, h].astype(jnp.float32)
            g = c * heads + h
            out_ref[:, :, g * HD : (g + 1) * HD] = total.astype(jnp.bfloat16)

    def finish(h, unused):
        dq_wait(h).wait_recv()
        dq_copy(h).wait_send()
        dq_local(h).wait()
        for copy in q_copies(h):
            copy.wait_send()
        kv_copy(h, 0, 1).wait_send()
        for d in range(1, depth + 1):
            @pl.when(direct(d))
            def _():
                for w in range(2):
                    kv_copy(h, d, w).wait_send()
        for step in range(1, depth):
            for w in range(2):
                pl.when(relays(step))(lambda: relay_copy(h, step, w).wait_send())
        def sent(slot):
            for t in range(1, sections):
                x_copy(h, slot, t).wait_send()

        for slot in range(blocks):
            when_block(slot, functools.partial(sent, slot))
            when_sent(slot, lambda: g_copy(h, slot).wait_send())
        return unused

    lax.fori_loop(0, heads, finish, 0)


def body(queries, grad_out, keys_values, doc_ids):
    layers, rows, width = queries.shape
    kv_width = keys_values.shape[2]
    heads_kv = kv_width // HD
    group = width // kv_width
    n = lax.axis_size("ctx")
    sections = lax.axis_size("section")
    reach = n // 4
    heads = heads_kv // 2
    blocks = reach + 2
    window = (reach + 1) * rows
    piece = rows // sections
    depth = reach // 2
    bf, f32 = jnp.bfloat16, jnp.float32
    dma = pltpu.SemaphoreType.DMA
    hbm = pl.BlockSpec(memory_space=pl.ANY)
    vmem = pl.BlockSpec(memory_space=pltpu.VMEM)
    grad_queries, grad_kv = pl.pallas_call(
        functools.partial(kernel, n, sections, reach, heads_kv, group),
        out_shape=(
            jax.ShapeDtypeStruct((layers * rows, width), bf),
            jax.ShapeDtypeStruct((2, piece, kv_width), bf),
        ),
        in_specs=[hbm, hbm, hbm, hbm],
        out_specs=(hbm, vmem),
        scratch_shapes=[
            pltpu.VMEM((n, rows), jnp.int32),
            pltpu.VMEM((heads, 2, layers * rows, group * HD), bf),
            pltpu.VMEM((heads, 2, layers * rows, group * HD), bf),
            pltpu.VMEM((heads, 2, blocks, rows, HD), bf),
            pltpu.VMEM((2, window, rows), f32),
            pltpu.VMEM((window, group * layers * rows), bf),
            pltpu.VMEM((heads, 2, window, group * layers * rows), bf),
            pltpu.VMEM((2, blocks * rows, HD), f32),
            pltpu.VMEM((heads, blocks, 2, rows, HD), bf),
            pltpu.VMEM((heads, blocks, max(sections - 1, 1), 2, piece, HD), bf),
            pltpu.VMEM((heads, blocks, 2, piece, HD), bf),
            pltpu.VMEM((depth + 1, 2, heads, 2, piece, HD), bf),
            pltpu.VMEM((heads, 2, layers * rows, group * HD), bf),
            dma,
            dma((heads, 3)),
            dma((heads, 2)),
            dma((heads, 2)),
            dma((heads, depth + 1, 2)),
            dma((heads, blocks)),
            dma((heads, max(depth - 1, 1), 2)),
            dma((heads, blocks, max(sections - 1, 1))),
            dma((heads, blocks, max(sections - 1, 1))),
            dma((heads, blocks)),
            dma((depth + 1, 2, heads)),
            dma((heads,)),
            dma((heads,)),
            dma((heads,)),
        ],
        compiler_params=pltpu.CompilerParams(
            collective_id=0, has_side_effects=True, vmem_limit_bytes=40 * 1024 * 1024
        ),
        name="cross_backward",
    )(
        *[
            pltpu.with_memory_space_constraint(x, pltpu.HBM)
            for x in (
                queries.reshape(layers * rows, width), grad_out.reshape(layers * rows, width),
                keys_values, doc_ids.reshape(n, rows),
            )
        ]
    )
    return grad_queries.reshape(queries.shape), grad_kv


def solution(mesh):
    return jax.shard_map(
        body,
        mesh=mesh,
        in_specs=(P("section", "ctx", None), P("section", "ctx", None), P(None, "ctx", None), P()),
        out_specs=(P("section", "ctx", None), P(None, ("ctx", "section"), None)),
        check_vma=False,
    )
```

```python
import functools

import jax
import jax.numpy as jnp
from jax import lax
from jax.experimental import pallas as pl
from jax.experimental.pallas import tpu as pltpu
from jax.sharding import PartitionSpec as P

HD = 128
MESH = pl.DeviceIdType.MESH
LOG2E = 1.4426950408889634
NEG = -1e30


def kernel(
    n, sections, reach, heads_kv, group,
    q_ref, do_ref, kv_ref, docs_ref,
    dq_ref, out_ref,
    docs, qbuf, dobuf, kvbuf, bias, pbuf, dsbuf, acc, sbuf, xbuf, tbuf, rbuf, dqbuf,
    docsem, lsem, qsend, qrecv, kvsend, kvrecv, relsend, xsend, xrecv, gsend, grecv, dqsend, dqrecv, dqloc,
):
    me = lax.axis_index("ctx")
    sec = lax.axis_index("section")
    rows = kv_ref.shape[1]
    layers = q_ref.shape[0] // rows
    core = lax.rem(me, 2)
    other = 1 - core
    chip = me // 2
    chips = n // 2
    depth = reach // 2
    place = lax.rem(chip, depth)
    blocks = reach + 2
    heads = heads_kv // 2
    gw = group * HD
    window = (reach + 1) * rows
    piece = rows // sections
    scale = HD ** (-0.5)

    def dev(ctx, section):
        return {"ctx": ctx, "section": section}

    def cols(head, width):
        return pl.ds(pl.multiple_of(head * width, HD), width)

    def local_copies(h):
        g = core * heads + h
        return [
            pltpu.make_async_copy(q_ref.at[:, cols(g, gw)], qbuf.at[h, core], lsem.at[h, 0]),
            pltpu.make_async_copy(do_ref.at[:, cols(g, gw)], dobuf.at[h, core], lsem.at[h, 1]),
            pltpu.make_async_copy(
                kv_ref.at[:, :, cols(g, HD)], kvbuf.at[h, :, reach + core], lsem.at[h, 2]
            ),
        ]

    def q_copies(h):
        g = other * heads + h
        partner = dev(2 * chip + other, sec)
        return [
            pltpu.make_async_remote_copy(
                src_ref=src.at[:, cols(g, gw)], dst_ref=dst.at[h, core],
                send_sem=qsend.at[h, k], recv_sem=qrecv.at[h, k],
                device_id=partner, device_id_type=MESH,
            )
            for k, (src, dst) in enumerate([(q_ref, qbuf), (do_ref, dobuf)])
        ]

    def kv_copy(h, d, w):
        to = lax.rem(core + w, 2)
        slot = core - 2 * d + reach
        return pltpu.make_async_remote_copy(
            src_ref=kv_ref.at[:, :, cols(to * heads + h, HD)], dst_ref=kvbuf.at[h, :, slot],
            send_sem=kvsend.at[h, d, w], recv_sem=kvrecv.at[h, slot],
            device_id=dev(2 * (chip + d) + to, sec), device_id_type=MESH,
        )

    def kv_wait(h, slot):
        return pltpu.make_async_remote_copy(
            src_ref=kv_ref.at[:, :, pl.ds(0, HD)], dst_ref=kvbuf.at[h, :, slot],
            send_sem=kvsend.at[h, 0, 0], recv_sem=kvrecv.at[h, slot],
            device_id=dev(2 * chip + other, sec), device_id_type=MESH,
        )

    def relay_copy(h, step, w):
        slot = 2 * step + w
        return pltpu.make_async_remote_copy(
            src_ref=kvbuf.at[h, :, w], dst_ref=kvbuf.at[h, :, slot],
            send_sem=relsend.at[h, step - 1, w], recv_sem=kvrecv.at[h, slot],
            device_id=dev(2 * (chip - step) + core, sec), device_id_type=MESH,
        )

    def direct(d):
        return (chip + d < chips) & (place + d < depth) if d < depth else chip + d < chips

    def relays(step):
        return (place >= step) & (chip >= depth)

    def relay(h):
        for w in range(2):
            @pl.when(chip >= depth)
            def _():
                kv_wait(h, w).wait_recv()
            for step in range(1, depth):
                pl.when(relays(step))(lambda: relay_copy(h, step, w).start())

    def x_copy(h, slot, t, k):
        to = lax.rem(sec + t, sections)
        return pltpu.make_async_remote_copy(
            src_ref=sbuf.at[h, slot, k, pl.ds(pl.multiple_of(to * piece, piece), piece)],
            dst_ref=xbuf.at[h, slot, t - 1, k],
            send_sem=xsend.at[h, slot, t - 1, k], recv_sem=xrecv.at[h, slot, t - 1, k],
            device_id=dev(me, to), device_id_type=MESH,
        )

    def g_copy(h, slot):
        d = (reach + 1 - slot) // 2
        return pltpu.make_async_remote_copy(
            src_ref=tbuf.at[h, slot], dst_ref=rbuf.at[d, core, h],
            send_sem=gsend.at[h, slot], recv_sem=grecv.at[d, core, h],
            device_id=dev(2 * (chip - d) + (slot - reach) % 2, sec), device_id_type=MESH,
        )

    def g_wait(h, d, c):
        return pltpu.make_async_remote_copy(
            src_ref=tbuf.at[h, 0], dst_ref=rbuf.at[d, c, h],
            send_sem=gsend.at[h, 0], recv_sem=grecv.at[d, c, h],
            device_id=dev(2 * chip + other, sec), device_id_type=MESH,
        )

    def when_block(slot, run):
        if slot < reach:
            pl.when(2 * chip - reach + slot >= 0)(run)
        else:
            run()

    def when_sent(slot, run):
        pl.when(2 * chip - reach + slot >= 0 if slot < reach else core != slot - reach)(run)

    def scatter(h, k, slots):
        def send(slot):
            for t in range(1, sections):
                x_copy(h, slot, t, k).start()

        for slot in slots:
            when_block(slot, functools.partial(send, slot))

    def deliver(h):
        own = pl.ds(pl.multiple_of(sec * piece, piece), piece)

        def run(slot):
            total = sbuf[h, slot, :, own].astype(jnp.float32)
            for t in range(1, sections):
                for k in range(2):
                    x_copy(h, slot, t, k).wait_recv()
                total = total + xbuf[h, slot, t - 1].astype(jnp.float32)
            tbuf[h, slot] = total.astype(jnp.bfloat16)
            when_sent(slot, lambda: g_copy(h, slot).start())

        for slot in range(blocks):
            when_block(slot, functools.partial(run, slot))
        rbuf[0, core, h] = tbuf[h, reach + core]

    def dq_copy(h):
        return pltpu.make_async_remote_copy(
            src_ref=dqbuf.at[h, other], dst_ref=dq_ref.at[:, cols(core * heads + h, gw)],
            send_sem=dqsend.at[h], recv_sem=dqrecv.at[h],
            device_id=dev(2 * chip + other, sec), device_id_type=MESH,
        )

    def dq_wait(h):
        return pltpu.make_async_remote_copy(
            src_ref=dqbuf.at[h, other], dst_ref=dq_ref.at[:, cols(other * heads + h, gw)],
            send_sem=dqsend.at[h], recv_sem=dqrecv.at[h],
            device_id=dev(2 * chip + other, sec), device_id_type=MESH,
        )

    def dq_local(h):
        return pltpu.make_async_copy(
            dqbuf.at[h, core], dq_ref.at[:, cols(core * heads + h, gw)], dqloc.at[h]
        )

    barrier = pltpu.get_barrier_semaphore()

    def greet(ctx, section):
        pl.semaphore_signal(barrier, inc=1, device_id=dev(ctx, section), device_id_type=MESH)

    for step in range(-depth, depth + 1):
        if abs(step) == depth:
            condition = (chip + step >= 0) & (chip + step < chips)
        else:
            condition = (place + step >= 0) & (place + step < depth)

        @pl.when(condition)
        def _():
            for w in range(2):
                if step == 0 and w == 0:
                    continue
                greet(2 * (chip + step) + lax.rem(core + w, 2), sec)

    for w in range(2):
        for t in range(1, sections):
            greet(2 * chip + lax.rem(core + w, 2), lax.rem(sec + t, sections))

    docs_copy = pltpu.make_async_copy(docs_ref, docs, docsem)
    docs_copy.start()
    for h in range(heads):
        for copy in local_copies(h):
            copy.start()

    near = depth + (chip >= depth).astype(jnp.int32) + (chip + depth < chips).astype(jnp.int32)
    pl.semaphore_wait(barrier, 2 * near - 1 + 2 * (sections - 1))

    for h in range(heads):
        for d in range(depth, 0, -1):
            @pl.when(direct(d))
            def _():
                for w in range(2):
                    kv_copy(h, d, w).start()
        kv_copy(h, 0, 1).start()
        for copy in q_copies(h):
            copy.start()

    for d in range(1, depth + 1):
        @pl.when(chip - d < 0)
        def _():
            for slot in (reach - 2 * d, reach - 2 * d + 1):
                for h in range(heads):
                    kvbuf[h, :, slot] = jnp.zeros((2, rows, HD), jnp.bfloat16)

        @pl.when(chip + d >= chips)
        def _():
            rbuf[d] = jnp.zeros(rbuf.shape[1:], jnp.bfloat16)

    docs_copy.wait()
    row_at = lax.broadcasted_iota(jnp.int32, (rows, rows), 0)
    col_at = lax.broadcasted_iota(jnp.int32, (rows, rows), 1)
    for slot in range(blocks):
        at = 2 * chip - reach + slot
        kdoc = docs[pl.ds(jnp.maximum(at, 0), 1), :].astype(jnp.float32)
        kdoc = jnp.transpose(jnp.broadcast_to(kdoc, (rows, rows)))
        for sub in range(2):
            if not 0 <= slot - sub <= reach:
                continue
            qdoc = docs[pl.ds(2 * chip + sub, 1), :].astype(jnp.float32)
            kplace = at * rows + row_at
            qplace = (2 * chip + sub) * rows + col_at
            seen = (kplace <= qplace) & (kplace >= 0) & (kdoc == qdoc)
            bias[sub, (slot - sub) * rows : (slot - sub + 1) * rows] = jnp.where(seen, 0.0, NEG)

    def score_part(h, sub):
        k = kvbuf[h, 0, pl.ds(sub, reach + 1)].reshape(window, HD)
        v = kvbuf[h, 1, pl.ds(sub, reach + 1)].reshape(window, HD)
        nt = (((1,), (1,)), ((), ()))
        for i in range(group):
            at = slice(i * HD, (i + 1) * HD)
            s = lax.dot_general(k, qbuf[h, sub, :, at], nt, preferred_element_type=jnp.float32)
            dp = lax.dot_general(v, dobuf[h, sub, :, at], nt, preferred_element_type=jnp.float32)
            s = s * (scale * LOG2E) + jnp.concatenate([bias[sub]] * layers, axis=1)
            e = jnp.exp2(s - jnp.max(s, axis=0, keepdims=True))
            inverse = 1.0 / jnp.sum(e, axis=0, keepdims=True)
            delta = jnp.sum(e * dp, axis=0, keepdims=True) * inverse
            p = (e * inverse).astype(jnp.bfloat16)
            to = slice(i * layers * rows, (i + 1) * layers * rows)
            pbuf[sub, :, to] = p
            dsbuf[h, sub, :, to] = (p.astype(jnp.float32) * (dp - delta)).astype(jnp.bfloat16)

    def key_part(h, k):
        for sub in (core, other):
            keys_at = pl.ds(pl.multiple_of(sub * rows, rows), window)
            weights, buf = ((dsbuf.at[h, sub], qbuf), (pbuf.at[sub], dobuf))[k]
            stack = jnp.concatenate(
                [buf[h, sub, :, i * HD : (i + 1) * HD] for i in range(group)], axis=0
            )
            acc[k, keys_at] += jnp.dot(weights[...], stack, preferred_element_type=jnp.float32)
        for slot in range(blocks):
            total = acc[k, slot * rows : (slot + 1) * rows]
            sbuf[h, slot, k] = (total * scale if k == 0 else total).astype(jnp.bfloat16)

    def query_part(h, sub):
        kt = jnp.transpose(kvbuf[h, 0, pl.ds(sub, reach + 1)].reshape(window, HD))
        dqt = jnp.dot(kt, dsbuf[h, sub], preferred_element_type=jnp.float32) * scale
        for i in range(group):
            dqbuf[h, sub, :, i * HD : (i + 1) * HD] = jnp.transpose(
                dqt[:, i * layers * rows : (i + 1) * layers * rows]
            ).astype(jnp.bfloat16)

    relay(0)

    def head_step(h, unused):
        local_copies(h)[2].wait()
        for slot in range(2, blocks):
            at = 2 * chip - reach + slot
            if slot < reach:
                condition = at >= 0
            else:
                condition = core != slot - reach

            @pl.when(condition)
            def _():
                kv_wait(h, slot).wait_recv()

        acc[...] = jnp.zeros_like(acc)
        for copy in local_copies(h)[:2]:
            copy.wait()
        score_part(h, core)

        @pl.when(h + 1 < heads)
        def _():
            relay(h + 1)

        for copy in q_copies(h):
            copy.wait_recv()
        score_part(h, other)
        key_part(h, 1)
        scatter(h, 1, range(reach))
        key_part(h, 0)
        scatter(h, 0, range(reach))
        for k in range(2):
            scatter(h, k, range(reach, blocks))
        return unused

    lax.fori_loop(0, heads, head_step, 0)

    def query_step(h, unused):
        query_part(h, other)
        dq_copy(h).start()
        query_part(h, core)
        dq_local(h).start()
        deliver(h)
        return unused

    lax.fori_loop(0, heads, query_step, 0)

    for h in range(heads):
        for c in range(2):
            for d in range(depth, -1, -1):
                pl.when(core != c if d == 0 else chip + d < chips)(lambda: g_wait(h, d, c).wait_recv())
            total = rbuf[0, c, h].astype(jnp.float32)
            for d in range(1, depth + 1):
                total = total + rbuf[d, c, h].astype(jnp.float32)
            g = c * heads + h
            out_ref[:, :, g * HD : (g + 1) * HD] = total.astype(jnp.bfloat16)

    def finish(h, unused):
        dq_wait(h).wait_recv()
        dq_copy(h).wait_send()
        dq_local(h).wait()
        for copy in q_copies(h):
            copy.wait_send()
        kv_copy(h, 0, 1).wait_send()
        for d in range(1, depth + 1):
            @pl.when(direct(d))
            def _():
                for w in range(2):
                    kv_copy(h, d, w).wait_send()
        for step in range(1, depth):
            for w in range(2):
                pl.when(relays(step))(lambda: relay_copy(h, step, w).wait_send())
        def sent(slot):
            for t in range(1, sections):
                for k in range(2):
                    x_copy(h, slot, t, k).wait_send()

        for slot in range(blocks):
            when_block(slot, functools.partial(sent, slot))
            when_sent(slot, lambda: g_copy(h, slot).wait_send())
        return unused

    lax.fori_loop(0, heads, finish, 0)


def body(queries, grad_out, keys_values, doc_ids):
    layers, rows, width = queries.shape
    kv_width = keys_values.shape[2]
    heads_kv = kv_width // HD
    group = width // kv_width
    n = lax.axis_size("ctx")
    sections = lax.axis_size("section")
    reach = n // 4
    heads = heads_kv // 2
    blocks = reach + 2
    window = (reach + 1) * rows
    piece = rows // sections
    depth = reach // 2
    bf, f32 = jnp.bfloat16, jnp.float32
    dma = pltpu.SemaphoreType.DMA
    hbm = pl.BlockSpec(memory_space=pl.ANY)
    vmem = pl.BlockSpec(memory_space=pltpu.VMEM)
    grad_queries, grad_kv = pl.pallas_call(
        functools.partial(kernel, n, sections, reach, heads_kv, group),
        out_shape=(
            jax.ShapeDtypeStruct((layers * rows, width), bf),
            jax.ShapeDtypeStruct((2, piece, kv_width), bf),
        ),
        in_specs=[hbm, hbm, hbm, hbm],
        out_specs=(hbm, vmem),
        scratch_shapes=[
            pltpu.VMEM((n, rows), jnp.int32),
            pltpu.VMEM((heads, 2, layers * rows, group * HD), bf),
            pltpu.VMEM((heads, 2, layers * rows, group * HD), bf),
            pltpu.VMEM((heads, 2, blocks, rows, HD), bf),
            pltpu.VMEM((2, window, rows), f32),
            pltpu.VMEM((2, window, group * layers * rows), bf),
            pltpu.VMEM((heads, 2, window, group * layers * rows), bf),
            pltpu.VMEM((2, blocks * rows, HD), f32),
            pltpu.VMEM((heads, blocks, 2, rows, HD), bf),
            pltpu.VMEM((heads, blocks, max(sections - 1, 1), 2, piece, HD), bf),
            pltpu.VMEM((heads, blocks, 2, piece, HD), bf),
            pltpu.VMEM((depth + 1, 2, heads, 2, piece, HD), bf),
            pltpu.VMEM((heads, 2, layers * rows, group * HD), bf),
            dma,
            dma((heads, 3)),
            dma((heads, 2)),
            dma((heads, 2)),
            dma((heads, depth + 1, 2)),
            dma((heads, blocks)),
            dma((heads, max(depth - 1, 1), 2)),
            dma((heads, blocks, max(sections - 1, 1), 2)),
            dma((heads, blocks, max(sections - 1, 1), 2)),
            dma((heads, blocks)),
            dma((depth + 1, 2, heads)),
            dma((heads,)),
            dma((heads,)),
            dma((heads,)),
        ],
        compiler_params=pltpu.CompilerParams(
            collective_id=0, has_side_effects=True, vmem_limit_bytes=40 * 1024 * 1024
        ),
        name="cross_backward",
    )(
        *[
            pltpu.with_memory_space_constraint(x, pltpu.HBM)
            for x in (
                queries.reshape(layers * rows, width), grad_out.reshape(layers * rows, width),
                keys_values, doc_ids.reshape(n, rows),
            )
        ]
    )
    return grad_queries.reshape(queries.shape), grad_kv


def solution(mesh):
    return jax.shard_map(
        body,
        mesh=mesh,
        in_specs=(P("section", "ctx", None), P("section", "ctx", None), P(None, "ctx", None), P()),
        out_specs=(P("section", "ctx", None), P(None, ("ctx", "section"), None)),
        check_vma=False,
    )
```
